256 devices in a mesh: freq: 16 (over x, z_hi), tmpl: 16 (over y, z_lo, core).
Axes of the slice: x: 4, y: 4, z: 8 (z_hi: 4, z_lo: 2; z = z_hi * 2 + z_lo), core: 2. Of those that a mesh axis runs over, the one named last changes fastest.
Arguments:
- strain_spectrum: float32 [2, 1024, 1024], P(None, 'freq', 'tmpl'), may hold values from -6 to 6
- bank_spectra: bfloat16 [128, 2, 1024, 1024], P('tmpl', None, 'freq'), may hold values from -0.0029296875 to 0.0029296875
Outputs:
- snr_peaks: float32 [128, 1048576], P('tmpl', 'freq')
The draws below stay inside these ranges and needn't reach their ends.
All inputs are finite; a program needn't handle non-finite values.
Results may differ from the reference program's by a relative error of at most 0.0031.
Values may be sent and summed in bfloat16 or wider, within the bound.
A program may use at most 64 MiB of HBM per device.

```python
import math
import jax
import jax.numpy as jnp
from jax import lax

FA = 1024
FB = 1024
WIN = 256
SAMPLES = 1048576
TEMPLATES = 128


def level_of(own_key, shape, shards, low, largest):
    def one(axis_at, parts):
        steps = jax.random.uniform(jax.random.fold_in(jax.random.fold_in(own_key, 6), axis_at), (parts,), jnp.float32, low / len(shards), largest / len(shards))
        return jnp.repeat(jnp.exp(steps), shape[axis_at] // parts).reshape((-1,) + (1,) * (len(shape) - axis_at - 1))

    gain = one(*shards[0])
    for cut in shards[1:]:
        gain = gain * one(*cut)
    return gain


def scatter_about(own_key, dims, scale, limit, pieces=(), kind=jnp.bfloat16):
    loudness = level_of(own_key, dims, pieces, -0.22, 0.18) if pieces else 1.0
    array = jax.random.normal(own_key, dims, jnp.float32) * scale * loudness
    return jnp.minimum(jnp.maximum(array, -limit), limit).astype(kind)


def setup_inputs(seed: int = 0) -> dict:
    arg_keys = jax.random.split(jax.random.key(seed), 3)
    strain_spectrum = scatter_about(arg_keys[0], (2, FA, FB), 1.0, 6.0, ((1, 16), (2, 16)), jnp.float32)
    bank_spectra = scatter_about(arg_keys[1], (TEMPLATES, 2, FA, FB), (4 * SAMPLES) ** -0.5, 0.0029296875, ((0, 16), (2, 16)))
    return dict(strain_spectrum=strain_spectrum, bank_spectra=bank_spectra)


def circle(length):
    ramp_index = jnp.arange(length, dtype=jnp.int32)
    angles = ((ramp_index[:, None] * ramp_index[None, :]) % length).astype(jnp.float32) * (2.0 * math.pi / length)
    return jnp.cos(angles), jnp.sin(angles)


def rotation(length):
    cosine_table, sine_table = circle(length)
    top_half = jnp.concatenate([cosine_table, sine_table], axis=1)
    low_half = jnp.concatenate([-sine_table, cosine_table], axis=1)
    return jnp.concatenate([top_half, low_half], axis=0).astype(jnp.bfloat16)


def twiddle(first_row, row_count, columns, period):
    row_index = first_row + jnp.arange(row_count, dtype=jnp.int32)
    ramp_index = jnp.arange(columns, dtype=jnp.int32)
    angles = (row_index[:, None] * ramp_index[None, :]).astype(jnp.float32) * (2.0 * math.pi / period)
    return jnp.cos(angles), jnp.sin(angles)


def sliding(padded, window):
    current = padded
    covered = 1
    while covered < window:
        stride = min(covered, window - covered)
        current = jnp.maximum(current[..., :-stride], current[..., stride:])
        covered = covered + stride
    return current


def reference(strain_spectrum, bank_spectra):
    forward_transform = rotation(FB)
    backward = rotation(FA)
    cosine_turn, sine_rotation = twiddle(0, FA, FB, SAMPLES)
    window_radius = WIN // 2

    def filter_one(template):
        spectrum = template.astype(jnp.float32)
        real_part = strain_spectrum[0] * spectrum[0] + strain_spectrum[1] * spectrum[1]
        imag_part = strain_spectrum[1] * spectrum[0] - strain_spectrum[0] * spectrum[1]
        cross_spectrum = jnp.concatenate([real_part, imag_part], axis=1).astype(jnp.bfloat16)
        initial_transform = jnp.dot(cross_spectrum, forward_transform, preferred_element_type=jnp.float32)
        first_real = initial_transform[:, :FB]
        first_imag = initial_transform[:, FB:]
        rotated_real = first_real * cosine_turn - first_imag * sine_rotation
        turned_imag = first_real * sine_rotation + first_imag * cosine_turn
        stacked = jnp.concatenate([rotated_real, turned_imag], axis=0).astype(jnp.bfloat16)
        second_pass = jnp.dot(stacked.T, backward, preferred_element_type=jnp.float32)
        energy = second_pass[:, :FA] ** 2 + second_pass[:, FA:] ** 2
        series = energy.T.reshape(SAMPLES)
        padded = jnp.concatenate([series[SAMPLES - window_radius:], series, series[:window_radius]])
        return sliding(padded, WIN)[:SAMPLES]

    return lax.map(filter_one, bank_spectra)
```

```python
import functools
import math

import jax
import jax.numpy as jnp
from jax import lax
from jax.experimental import pallas as pl
from jax.experimental.pallas import tpu as pltpu
from jax.sharding import PartitionSpec as P

WIN = 256
LANES = 128
CHUNK = 256
HALO = 16
MESH = pl.DeviceIdType.MESH


def unit_circle(index, bits):
    shift = bits - 2
    quarter = (index + (1 << (shift - 1))) >> shift
    rest = index - (quarter << shift)
    angle = rest.astype(jnp.float32) * (2.0 * math.pi / (1 << bits))
    square = angle * angle
    sine = angle * (
        1.0 + square * (-1.0 / 6 + square * (1.0 / 120 + square * (-1.0 / 5040 + square * (1.0 / 362880))))
    )
    cosine = 1.0 + square * (
        -0.5 + square * (1.0 / 24 + square * (-1.0 / 720 + square * (1.0 / 40320 + square * (-1.0 / 3628800))))
    )
    odd = (quarter & 1) == 1
    cos_value = jnp.where(odd, sine, cosine)
    sin_value = jnp.where(odd, cosine, sine)
    cos_value = jnp.where(((quarter + 1) & 2) == 2, -cos_value, cos_value)
    sin_value = jnp.where((quarter & 2) == 2, -sin_value, sin_value)
    return cos_value, sin_value


def iotas(shape):
    return lax.broadcasted_iota(jnp.int32, shape, 0), lax.broadcasted_iota(jnp.int32, shape, 1)


def kernel(
    dims,
    strain_ref,
    bank_ref,
    out_ref,
    bank,
    near_c,
    near_s,
    far_c,
    far_s,
    cos_table,
    sin_table,
    turn_c,
    turn_s,
    packed,
    gathered,
    strain_re,
    strain_im,
    product,
    turned,
    spectra,
    energy,
    series,
    halo,
    result,
    bank_sem,
    out_sem,
    strain_send,
    strain_recv,
    turned_send,
    turned_recv,
    energy_send,
    energy_recv,
    halo_send,
    halo_recv,
):
    groups, members, rows, columns, steps, halves, blocks = dims
    bits = columns.bit_length() - 1
    height = rows * groups
    f = lax.axis_index("freq")
    t = lax.axis_index("tmpl")
    flipped = t + 2 - 4 * ((t // 2) % 2)
    my_half = f // blocks
    my_block = f % blocks

    def partner(j):
        return ((f // 4 + j // 4) % 4) * 4 + (f % 4 + j % 4) % 4

    barrier = pltpu.get_barrier_semaphore()

    def greet(j, carry):
        pl.semaphore_signal(barrier, inc=1, device_id=(f, (t + j) % members), device_id_type=MESH)
        pl.semaphore_signal(barrier, inc=1, device_id=(partner(j), flipped), device_id_type=MESH)
        return carry

    lax.fori_loop(1, groups, greet, 0)

    bank_copy = pltpu.make_async_copy(bank_ref, bank, bank_sem)
    bank_copy.start()
    packed[...] = jnp.concatenate([strain_ref[0], strain_ref[1]], axis=1)

    row, col = iotas((rows, columns))
    near_c[...], near_s[...] = unit_circle((row * col) & (columns - 1), bits)
    row, col = iotas((groups, columns))
    far_c[...], far_s[...] = unit_circle((row * col * rows) & (columns - 1), bits)

    def table(h, carry):
        fc = far_c[pl.ds(h, 1), :]
        fs = far_s[pl.ds(h, 1), :]
        nc = near_c[...]
        ns = near_s[...]
        at = pl.ds(pl.multiple_of(h * rows, rows), rows)
        cos_table[at, :] = (nc * fc - ns * fs).astype(jnp.bfloat16)
        sin_table[at, :] = (ns * fc + nc * fs).astype(jnp.bfloat16)
        return carry

    lax.fori_loop(0, groups, table, 0)

    pl.semaphore_wait(barrier, 2 * (groups - 1))

    def send_strain(j, carry):
        pltpu.make_async_remote_copy(
            src_ref=packed,
            dst_ref=gathered.at[t],
            send_sem=strain_send,
            recv_sem=strain_recv,
            device_id=(f, (t + j) % members),
            device_id_type=MESH,
        ).start()
        return carry

    lax.fori_loop(1, members, send_strain, 0)
    gathered[t] = packed[...]

    row, col = iotas((rows, columns))
    turn_c[...], turn_s[...] = unit_circle((f * rows + row) * col, 2 * bits)

    others = gathered.at[pl.ds(0, members - 1)]
    pltpu.make_async_copy(others, others, strain_recv).wait()
    lane = lax.broadcasted_iota(jnp.int32, (rows, LANES), 1)
    low = lane < LANES // 2
    for pair in range(members // 2):
        first = gathered[2 * pair]
        second = gathered[2 * pair + 1]
        at = pl.ds(pair * LANES, LANES)
        strain_re[:, at] = jnp.where(low, first, pltpu.roll(second, LANES // 2, 1))
        strain_im[:, at] = jnp.where(low, pltpu.roll(first, LANES // 2, 1), second)
    bank_copy.wait()

    def first_pass(i, carry):
        sr = strain_re[...]
        si = strain_im[...]
        for h in range(halves):
            hr = bank[h * steps + i, 0].astype(jnp.float32)
            hi = bank[h * steps + i, 1].astype(jnp.float32)
            product[pl.ds(h * rows, rows), :] = (sr * hr + si * hi).astype(jnp.bfloat16)
            product[pl.ds((halves + h) * rows, rows), :] = (si * hr - sr * hi).astype(jnp.bfloat16)

        def columns_of(n, inner):
            at = pl.ds(pl.multiple_of(n * CHUNK, CHUNK), CHUNK)
            with_cos = jnp.dot(product[...], cos_table[:, at], preferred_element_type=jnp.float32)
            with_sin = jnp.dot(product[...], sin_table[:, at], preferred_element_type=jnp.float32)
            tc = turn_c[:, at]
            ts = turn_s[:, at]
            for h in range(halves):
                up = slice(h * rows, (h + 1) * rows)
                down = slice((halves + h) * rows, (halves + h + 1) * rows)
                re = with_cos[up] - with_sin[down]
                im = with_sin[up] + with_cos[down]
                turned_re = (re * tc - im * ts).astype(jnp.bfloat16)
                turned_im = (re * ts + im * tc).astype(jnp.bfloat16)
                for q in range(CHUNK // LANES):
                    piece = slice(q * LANES, (q + 1) * LANES)
                    d = h * blocks + n * (CHUNK // LANES) + q
                    turned[i, d, :, :LANES] = turned_re[:, piece]
                    turned[i, d, :, LANES:] = turned_im[:, piece]
            return inner

        lax.fori_loop(0, columns // CHUNK, columns_of, 0)

        def send(j, inner):
            d = partner(j)
            pltpu.make_async_remote_copy(
                src_ref=turned.at[i, d],
                dst_ref=spectra.at[i, pl.ds(pl.multiple_of(f * rows, rows), rows)],
                send_sem=turned_send.at[i],
                recv_sem=turned_recv.at[i],
                device_id=(d, flipped),
                device_id_type=MESH,
            ).start()
            return inner

        lax.fori_loop(0, groups, send, 0)
        return carry

    lax.fori_loop(0, steps, first_pass, 0)

    def second_pass(i, carry):
        here = spectra.at[i]
        pltpu.make_async_copy(here, here, turned_recv.at[i]).wait()

        def rows_of(n, inner):
            at = pl.ds(pl.multiple_of(n * CHUNK, CHUNK), CHUNK)
            with_cos = jnp.dot(cos_table[at, :], spectra[i], preferred_element_type=jnp.float32)
            with_sin = jnp.dot(sin_table[at, :], spectra[i], preferred_element_type=jnp.float32)
            re = with_cos[:, :LANES] - with_sin[:, LANES:]
            im = with_sin[:, :LANES] + with_cos[:, LANES:]
            energy[i, at, :] = (re * re + im * im).astype(jnp.bfloat16)
            return inner

        lax.fori_loop(0, height // CHUNK, rows_of, 0)

        def send(j, inner):
            d = partner(j)
            pltpu.make_async_remote_copy(
                src_ref=energy.at[i, pl.ds(pl.multiple_of(d * rows, rows), rows)],
                dst_ref=series.at[i, f],
                send_sem=energy_send.at[i],
                recv_sem=energy_recv.at[i],
                device_id=(d, flipped),
                device_id_type=MESH,
            ).start()

            @pl.when(my_block == blocks - 1)
            def _():
                start = pl.multiple_of((d * rows + height - HALO) % height, HALO)
                pltpu.make_async_remote_copy(
                    src_ref=energy.at[i, pl.ds(start, HALO)],
                    dst_ref=halo.at[i, my_half, 0],
                    send_sem=halo_send.at[i],
                    recv_sem=halo_recv.at[i],
                    device_id=(d, flipped),
                    device_id_type=MESH,
                ).start()

            @pl.when(my_block == 0)
            def _():
                start = pl.multiple_of(((d + 1) * rows) % height, HALO)
                pltpu.make_async_remote_copy(
                    src_ref=energy.at[i, pl.ds(start, HALO)],
                    dst_ref=halo.at[i, my_half, 1],
                    send_sem=halo_send.at[i],
                    recv_sem=halo_recv.at[i],
                    device_id=(d, flipped),
                    device_id_type=MESH,
                ).start()

            return inner

        lax.fori_loop(0, groups, send, 0)
        return carry

    lax.fori_loop(0, steps, second_pass, 0)

    def window(i, carry):
        here = series.at[i]
        pltpu.make_async_copy(here, here, energy_recv.at[i]).wait()
        edges = halo.at[i]
        pltpu.make_async_copy(edges, edges, halo_recv.at[i]).wait()

        def one(h, inner):
            before = halo[i, h, 0].astype(jnp.float32)[HALO - 8 :]
            after = halo[i, h, 1].astype(jnp.float32)[:8]
            tiles = [series[i, h * blocks + b].astype(jnp.float32) for b in range(blocks)]
            follow = jnp.concatenate([after, tiles[0], after], axis=0)
            follow = pltpu.roll(follow, rows + 15, 0)[: rows + 8]
            tiles = [jnp.concatenate([before, tile], axis=0) for tile in tiles] + [follow]
            place = lax.broadcasted_iota(jnp.int32, (rows + 8, LANES), 1)
            stride = 1
            while stride < LANES:
                moved = [pltpu.roll(tile, LANES - stride, 1) for tile in tiles]
                inside = place < LANES - stride
                tiles = [
                    jnp.maximum(tiles[b], jnp.where(inside, moved[b], moved[b + 1])) for b in range(blocks)
                ] + [jnp.maximum(tiles[blocks], moved[blocks])]
                stride *= 2
            ahead = pltpu.roll(tiles[blocks - 1], 1, 0)[8:]
            for b in range(blocks):
                peak = jnp.maximum(ahead, tiles[b][8:])
                ahead = tiles[b][8:]
                result[pl.ds(b * 8 + h * steps + i, rows, stride=8 * blocks), :] = peak
            return inner

        lax.fori_loop(0, halves, one, 0)
        return carry

    lax.fori_loop(0, steps, window, 0)

    out_copy = pltpu.make_async_copy(result, out_ref, out_sem)
    out_copy.start()
    pltpu.make_async_copy(others, others, strain_send).wait()

    def drain(i, carry):
        sent = turned.at[i]
        pltpu.make_async_copy(sent, sent, turned_send.at[i]).wait()
        sent = series.at[i]
        pltpu.make_async_copy(sent, sent, energy_send.at[i]).wait()

        @pl.when((my_block == 0) | (my_block == blocks - 1))
        def _():
            edge = energy.at[i, pl.ds(0, groups * HALO)]
            pltpu.make_async_copy(edge, edge, halo_send.at[i]).wait()

        return carry

    lax.fori_loop(0, steps, drain, 0)
    out_copy.wait()


def shards(groups, members, strain_spectrum, bank_spectra):
    templates, _, rows, columns = bank_spectra.shape
    blocks = columns // LANES
    halves = groups // blocks
    steps = templates // halves
    height = rows * groups
    dims = (groups, members, rows, columns, steps, halves, blocks)
    f32, bf16 = jnp.float32, jnp.bfloat16
    dma = pltpu.SemaphoreType.DMA
    out = pl.pallas_call(
        functools.partial(kernel, dims),
        out_shape=jax.ShapeDtypeStruct((rows * blocks * templates, LANES), f32),
        in_specs=[pl.BlockSpec(memory_space=pltpu.VMEM), pl.BlockSpec(memory_space=pl.ANY)],
        out_specs=pl.BlockSpec(memory_space=pl.ANY),
        scratch_shapes=[
            pltpu.VMEM((templates, 2, rows, columns), bf16),
            pltpu.VMEM((rows, columns), f32),
            pltpu.VMEM((rows, columns), f32),
            pltpu.VMEM((groups, columns), f32),
            pltpu.VMEM((groups, columns), f32),
            pltpu.VMEM((columns, columns), bf16),
            pltpu.VMEM((columns, columns), bf16),
            pltpu.VMEM((rows, columns), f32),
            pltpu.VMEM((rows, columns), f32),
            pltpu.VMEM((rows, LANES), f32),
            pltpu.VMEM((members, rows, LANES), f32),
            pltpu.VMEM((rows, columns), f32),
            pltpu.VMEM((rows, columns), f32),
            pltpu.VMEM((2 * halves * rows, columns), bf16),
            pltpu.VMEM((steps, groups, rows, 2 * LANES), bf16),
            pltpu.VMEM((steps, height, 2 * LANES), bf16),
            pltpu.VMEM((steps, height, LANES), bf16),
            pltpu.VMEM((steps, groups, rows, LANES), bf16),
            pltpu.VMEM((steps, halves, 2, HALO, LANES), bf16),
            pltpu.VMEM((rows * blocks * templates, LANES), f32),
            dma,
            dma,
            dma,
            dma,
            dma((steps,)),
            dma((steps,)),
            dma((steps,)),
            dma((steps,)),
            dma((steps,)),
            dma((steps,)),
        ],
        compiler_params=pltpu.CompilerParams(
            collective_id=0, has_side_effects=True, vmem_limit_bytes=40 * 2**20
        ),
    )(strain_spectrum, bank_spectra)
    out = out.reshape(rows * blocks, templates, LANES).transpose(1, 0, 2)
    return out.reshape(templates, rows * columns)


def solution(mesh):
    body = functools.partial(shards, mesh.shape["freq"], mesh.shape["tmpl"])
    in_specs = (P(None, "freq", "tmpl"), P("tmpl", None, "freq", None))
    return jax.shard_map(body, mesh=mesh, in_specs=in_specs, out_specs=P("tmpl", "freq"), check_vma=False)
```

```python
import functools
import math

import jax
import jax.numpy as jnp
from jax import lax
from jax.experimental import pallas as pl
from jax.experimental.pallas import tpu as pltpu
from jax.sharding import PartitionSpec as P

LANES = 128
CHUNK = 256
HALO = 16
MESH = pl.DeviceIdType.MESH


def unit_circle(index, bits):
    shift = bits - 2
    quarter = (index + (1 << (shift - 1))) >> shift
    rest = index - (quarter << shift)
    angle = rest.astype(jnp.float32) * (2.0 * math.pi / (1 << bits))
    square = angle * angle
    sine = angle * (
        1.0 + square * (-1.0 / 6 + square * (1.0 / 120 + square * (-1.0 / 5040 + square * (1.0 / 362880))))
    )
    cosine = 1.0 + square * (
        -0.5 + square * (1.0 / 24 + square * (-1.0 / 720 + square * (1.0 / 40320 + square * (-1.0 / 3628800))))
    )
    odd = (quarter & 1) == 1
    cos_value = jnp.where(odd, sine, cosine)
    sin_value = jnp.where(odd, cosine, sine)
    cos_value = jnp.where(((quarter + 1) & 2) == 2, -cos_value, cos_value)
    sin_value = jnp.where((quarter & 2) == 2, -sin_value, sin_value)
    return cos_value, sin_value


def iotas(shape):
    return lax.broadcasted_iota(jnp.int32, shape, 0), lax.broadcasted_iota(jnp.int32, shape, 1)


def kernel(
    dims,
    strain_ref,
    bank_ref,
    result,
    strain,
    bank,
    near_c,
    near_s,
    far_c,
    far_s,
    cos_table,
    sin_table,
    turn_c,
    turn_s,
    packed,
    gathered,
    strain_re,
    strain_im,
    product,
    turned,
    spectra,
    energy,
    series,
    halo,
    strain_sem,
    bank_sem,
    strain_send,
    strain_recv,
    sibling_recv,
    turned_send,
    turned_recv,
    energy_send,
    energy_recv,
    halo_send,
    halo_recv,
):
    groups, members, rows, columns, steps, halves, blocks = dims
    bits = columns.bit_length() - 1
    height = rows * groups
    f = lax.axis_index("freq")
    t = lax.axis_index("tmpl")
    flipped = t + 2 - 4 * ((t // 2) % 2)
    sibling = t + 1 - 2 * (t % 2)
    pairs = members // 2
    slot = (t % 2) * pairs + t // 2
    my_half = f // blocks
    my_block = f % blocks

    def partner(j):
        return ((f // 4 + j // 4) % 4) * 4 + (f % 4 + j % 4) % 4

    strain_copy = pltpu.make_async_copy(strain_ref, strain, strain_sem)
    strain_copy.start()
    barrier = pltpu.get_barrier_semaphore()

    def greet_partner(j, carry):
        pl.semaphore_signal(barrier, inc=1, device_id=(partner(j), flipped), device_id_type=MESH)
        return carry

    def greet_member(j, carry):
        pl.semaphore_signal(barrier, inc=1, device_id=(f, (t + 2 * j) % members), device_id_type=MESH)
        return carry

    lax.fori_loop(1, groups, greet_partner, 0)
    lax.fori_loop(1, pairs, greet_member, 0)
    pl.semaphore_signal(barrier, inc=1, device_id=(f, sibling), device_id_type=MESH)

    bank_copy = pltpu.make_async_copy(bank_ref, bank, bank_sem)
    bank_copy.start()

    row, col = iotas((rows, columns))
    near_c[...], near_s[...] = unit_circle((row * col) & (columns - 1), bits)
    row, col = iotas((groups, columns))
    far_c[...], far_s[...] = unit_circle((row * col * rows) & (columns - 1), bits)

    def table(h, carry):
        fc = far_c[pl.ds(h, 1), :]
        fs = far_s[pl.ds(h, 1), :]
        nc = near_c[...]
        ns = near_s[...]
        at = pl.ds(pl.multiple_of(h * rows, rows), rows)
        cos_table[at, :] = (nc * fc - ns * fs).astype(jnp.bfloat16)
        sin_table[at, :] = (ns * fc + nc * fs).astype(jnp.bfloat16)
        return carry

    strain_copy.wait()
    packed[...] = jnp.concatenate([strain[0], strain[1]], axis=1)
    pl.semaphore_wait(barrier, groups - 1 + pairs)

    def send_strain(j, carry):
        pltpu.make_async_remote_copy(
            src_ref=packed,
            dst_ref=gathered.at[slot],
            send_sem=strain_send,
            recv_sem=strain_recv.at[j],
            device_id=(f, (t + 2 * j) % members),
            device_id_type=MESH,
        ).start()
        return carry

    lax.fori_loop(1, pairs, send_strain, 0)
    pltpu.make_async_remote_copy(
        src_ref=packed,
        dst_ref=gathered.at[slot],
        send_sem=strain_send,
        recv_sem=sibling_recv,
        device_id=(f, sibling),
        device_id_type=MESH,
    ).start()
    gathered[slot] = packed[...]
    per_pair = groups // pairs
    lax.fori_loop(0, per_pair, table, 0)

    def forward(j, carry):
        lax.fori_loop(per_pair * j, per_pair * (j + 1), table, 0)
        source = (t - 2 * j + members) % members
        block = gathered.at[(t % 2) * pairs + source // 2]
        pltpu.make_async_copy(block, block, strain_recv.at[j]).wait()
        pltpu.make_async_remote_copy(
            src_ref=block,
            dst_ref=block,
            send_sem=strain_send,
            recv_sem=sibling_recv,
            device_id=(f, sibling),
            device_id_type=MESH,
        ).start()
        return carry

    lax.fori_loop(1, pairs, forward, 0)

    row, col = iotas((rows, columns))
    turn_c[...], turn_s[...] = unit_circle((f * rows + row) * col, 2 * bits)

    sent = gathered.at[pl.ds(0, members - 1)]
    half = gathered.at[pl.ds(pl.multiple_of((1 - t % 2) * pairs, pairs), pairs)]
    pltpu.make_async_copy(half, half, sibling_recv).wait()
    lane = lax.broadcasted_iota(jnp.int32, (rows, LANES), 1)
    low = lane < LANES // 2
    for pair in range(members // 2):
        first = gathered[pair]
        second = gathered[pairs + pair]
        at = pl.ds(pair * LANES, LANES)
        strain_re[:, at] = jnp.where(low, first, pltpu.roll(second, LANES // 2, 1))
        strain_im[:, at] = jnp.where(low, pltpu.roll(first, LANES // 2, 1), second)
    bank_copy.wait()

    def first_pass(i, carry):
        sr = strain_re[...]
        si = strain_im[...]
        for h in range(halves):
            hr = bank[h * steps + i, 0].astype(jnp.float32)
            hi = bank[h * steps + i, 1].astype(jnp.float32)
            product[pl.ds(h * rows, rows), :] = (sr * hr + si * hi).astype(jnp.bfloat16)
            product[pl.ds((halves + h) * rows, rows), :] = (si * hr - sr * hi).astype(jnp.bfloat16)

        def columns_of(j, inner):
            n = (my_block // 2 + j) % (columns // CHUNK)
            at = pl.ds(pl.multiple_of(n * CHUNK, CHUNK), CHUNK)
            with_cos = jnp.dot(product[...], cos_table[:, at], preferred_element_type=jnp.float32)
            with_sin = jnp.dot(product[...], sin_table[:, at], preferred_element_type=jnp.float32)
            tc = turn_c[:, at]
            ts = turn_s[:, at]
            for h in range(halves):
                up = slice(h * rows, (h + 1) * rows)
                down = slice((halves + h) * rows, (halves + h + 1) * rows)
                re = with_cos[up] - with_sin[down]
                im = with_sin[up] + with_cos[down]
                turned_re = (re * tc - im * ts).astype(jnp.bfloat16)
                turned_im = (re * ts + im * tc).astype(jnp.bfloat16)
                for q in range(CHUNK // LANES):
                    piece = slice(q * LANES, (q + 1) * LANES)
                    d = h * blocks + n * (CHUNK // LANES) + q
                    turned[i, d, :, :LANES] = turned_re[:, piece]
                    turned[i, d, :, LANES:] = turned_im[:, piece]
            for h in range(halves):
                for q in range(CHUNK // LANES):
                    d = h * blocks + n * (CHUNK // LANES) + q
                    pltpu.make_async_remote_copy(
                        src_ref=turned.at[i, d],
                        dst_ref=spectra.at[i, pl.ds(pl.multiple_of(f * rows, rows), rows)],
                        send_sem=turned_send.at[i],
                        recv_sem=turned_recv.at[i],
                        device_id=(d, flipped),
                        device_id_type=MESH,
                    ).start()
            return inner

        lax.fori_loop(0, columns // CHUNK, columns_of, 0)
        return carry

    lax.fori_loop(0, steps, first_pass, 0)

    def second_pass(i, carry):
        here = spectra.at[i]
        pltpu.make_async_copy(here, here, turned_recv.at[i]).wait()

        def rows_of(n, inner):
            at = pl.ds(pl.multiple_of(n * CHUNK, CHUNK), CHUNK)
            with_cos = jnp.dot(cos_table[at, :], spectra[i], preferred_element_type=jnp.float32)
            with_sin = jnp.dot(sin_table[at, :], spectra[i], preferred_element_type=jnp.float32)
            re = with_cos[:, :LANES] - with_sin[:, LANES:]
            im = with_sin[:, :LANES] + with_cos[:, LANES:]
            energy[i, at, :] = (re * re + im * im).astype(jnp.bfloat16)
            return inner

        lax.fori_loop(0, height // CHUNK, rows_of, 0)

        def send(j, inner):
            d = partner(j)
            pltpu.make_async_remote_copy(
                src_ref=energy.at[i, pl.ds(pl.multiple_of(d * rows, rows), rows)],
                dst_ref=series.at[i, f],
                send_sem=energy_send.at[i],
                recv_sem=energy_recv.at[i],
                device_id=(d, flipped),
                device_id_type=MESH,
            ).start()

            @pl.when(my_block == blocks - 1)
            def _():
                start = pl.multiple_of((d * rows + height - HALO) % height, HALO)
                pltpu.make_async_remote_copy(
                    src_ref=energy.at[i, pl.ds(start, HALO)],
                    dst_ref=halo.at[i, my_half, 0],
                    send_sem=halo_send.at[i],
                    recv_sem=halo_recv.at[i],
                    device_id=(d, flipped),
                    device_id_type=MESH,
                ).start()

            @pl.when(my_block == 0)
            def _():
                start = pl.multiple_of(((d + 1) * rows) % height, HALO)
                pltpu.make_async_remote_copy(
                    src_ref=energy.at[i, pl.ds(start, HALO)],
                    dst_ref=halo.at[i, my_half, 1],
                    send_sem=halo_send.at[i],
                    recv_sem=halo_recv.at[i],
                    device_id=(d, flipped),
                    device_id_type=MESH,
                ).start()

            return inner

        lax.fori_loop(0, groups, send, 0)
        return carry

    lax.fori_loop(0, steps, second_pass, 0)

    def window(i, carry):
        here = series.at[i]
        pltpu.make_async_copy(here, here, energy_recv.at[i]).wait()
        edges = halo.at[i]
        pltpu.make_async_copy(edges, edges, halo_recv.at[i]).wait()

        def one(h, inner):
            before = halo[i, h, 0].astype(jnp.float32)[HALO - 8 :]
            after = halo[i, h, 1].astype(jnp.float32)[:8]
            tiles = [series[i, h * blocks + b].astype(jnp.float32) for b in range(blocks)]
            follow = jnp.concatenate([after, tiles[0], after], axis=0)
            follow = pltpu.roll(follow, rows + 15, 0)[: rows + 8]
            tiles = [jnp.concatenate([before, tile], axis=0) for tile in tiles] + [follow]
            place = lax.broadcasted_iota(jnp.int32, (rows + 8, LANES), 1)
            stride = 1
            while stride < LANES:
                moved = [pltpu.roll(tile, LANES - stride, 1) for tile in tiles]
                inside = place < LANES - stride
                tiles = [
                    jnp.maximum(tiles[b], jnp.where(inside, moved[b], moved[b + 1])) for b in range(blocks)
                ] + [jnp.maximum(tiles[blocks], moved[blocks])]
                stride *= 2
            ahead = pltpu.roll(tiles[blocks - 1], 1, 0)[8:]
            for b in range(blocks):
                peak = jnp.maximum(ahead, tiles[b][8:])
                ahead = tiles[b][8:]
                result[pl.ds(b * 8 + h * steps + i, rows, stride=8 * blocks), :] = peak
            return inner

        lax.fori_loop(0, halves, one, 0)
        return carry

    lax.fori_loop(0, steps, window, 0)

    pltpu.make_async_copy(sent, sent, strain_send).wait()

    def drain(i, carry):
        out = turned.at[i]
        pltpu.make_async_copy(out, out, turned_send.at[i]).wait()
        out = series.at[i]
        pltpu.make_async_copy(out, out, energy_send.at[i]).wait()

        @pl.when((my_block == 0) | (my_block == blocks - 1))
        def _():
            edge = energy.at[i, pl.ds(0, groups * HALO)]
            pltpu.make_async_copy(edge, edge, halo_send.at[i]).wait()

        return carry

    lax.fori_loop(0, steps, drain, 0)


def shards(groups, members, strain_spectrum, bank_spectra):
    templates, _, rows, columns = bank_spectra.shape
    blocks = columns // LANES
    halves = groups // blocks
    steps = templates // halves
    height = rows * groups
    dims = (groups, members, rows, columns, steps, halves, blocks)
    f32, bf16 = jnp.float32, jnp.bfloat16
    dma = pltpu.SemaphoreType.DMA
    out = pl.pallas_call(
        functools.partial(kernel, dims),
        out_shape=jax.ShapeDtypeStruct((rows * blocks * templates, LANES), f32),
        in_specs=[pl.BlockSpec(memory_space=pltpu.HBM)] * 2,
        out_specs=pl.BlockSpec(memory_space=pltpu.VMEM),
        scratch_shapes=[
            pltpu.VMEM((2, rows, columns // members), f32),
            pltpu.VMEM((templates, 2, rows, columns), bf16),
            pltpu.VMEM((rows, columns), f32),
            pltpu.VMEM((rows, columns), f32),
            pltpu.VMEM((groups, columns), f32),
            pltpu.VMEM((groups, columns), f32),
            pltpu.VMEM((columns, columns), bf16),
            pltpu.VMEM((columns, columns), bf16),
            pltpu.VMEM((rows, columns), f32),
            pltpu.VMEM((rows, columns), f32),
            pltpu.VMEM((rows, LANES), f32),
            pltpu.VMEM((members, rows, LANES), f32),
            pltpu.VMEM((rows, columns), f32),
            pltpu.VMEM((rows, columns), f32),
            pltpu.VMEM((2 * halves * rows, columns), bf16),
            pltpu.VMEM((steps, groups, rows, 2 * LANES), bf16),
            pltpu.VMEM((steps, height, 2 * LANES), bf16),
            pltpu.VMEM((steps, height, LANES), bf16),
            pltpu.VMEM((steps, groups, rows, LANES), bf16),
            pltpu.VMEM((steps, halves, 2, HALO, LANES), bf16),
            dma,
            dma,
            dma,
            dma((members // 2,)),
            dma,
            dma((steps,)),
            dma((steps,)),
            dma((steps,)),
            dma((steps,)),
            dma((steps,)),
            dma((steps,)),
        ],
        compiler_params=pltpu.CompilerParams(
            collective_id=0, has_side_effects=True, vmem_limit_bytes=40 * 2**20
        ),
    )(*[pltpu.with_memory_space_constraint(x, pltpu.HBM) for x in (strain_spectrum, bank_spectra)])
    out = out.reshape(rows * blocks, templates, LANES).transpose(1, 0, 2)
    return out.reshape(templates, rows * columns)


def solution(mesh):
    body = functools.partial(shards, mesh.shape["freq"], mesh.shape["tmpl"])
    in_specs = (P(None, "freq", "tmpl"), P("tmpl", None, "freq", None))
    return jax.shard_map(body, mesh=mesh, in_specs=in_specs, out_specs=P("tmpl", "freq"), check_vma=False)
```

```python
import functools
import math

import jax
import jax.numpy as jnp
from jax import lax
from jax.experimental import pallas as pl
from jax.experimental.pallas import tpu as pltpu
from jax.sharding import PartitionSpec as P

LANES = 128
CHUNK = 256
MESH = pl.DeviceIdType.MESH


def unit_circle(index, bits):
    shift = bits - 2
    quarter = (index + (1 << (shift - 1))) >> shift
    rest = index - (quarter << shift)
    angle = rest.astype(jnp.float32) * (2.0 * math.pi / (1 << bits))
    square = angle * angle
    sine = angle * (
        1.0 + square * (-1.0 / 6 + square * (1.0 / 120 + square * (-1.0 / 5040 + square * (1.0 / 362880))))
    )
    cosine = 1.0 + square * (
        -0.5 + square * (1.0 / 24 + square * (-1.0 / 720 + square * (1.0 / 40320 + square * (-1.0 / 3628800))))
    )
    odd = (quarter & 1) == 1
    cos_value = jnp.where(odd, sine, cosine)
    sin_value = jnp.where(odd, cosine, sine)
    cos_value = jnp.where(((quarter + 1) & 2) == 2, -cos_value, cos_value)
    sin_value = jnp.where((quarter & 2) == 2, -sin_value, sin_value)
    return cos_value, sin_value


def iotas(shape):
    return lax.broadcasted_iota(jnp.int32, shape, 0), lax.broadcasted_iota(jnp.int32, shape, 1)


def kernel(
    dims,
    strain_ref,
    bank_ref,
    result,
    strain,
    bank,
    near_c,
    near_s,
    far_c,
    far_s,
    cos_table,
    sin_table,
    turn_c,
    turn_s,
    packed,
    gathered,
    strain_re,
    strain_im,
    product,
    turned,
    spectra,
    energy,
    series,
    edges,
    halo,
    strain_sem,
    bank_sem,
    strain_send,
    strain_recv,
    sibling_recv,
    turned_send,
    turned_recv,
    energy_send,
    energy_recv,
    halo_send,
    halo_recv,
):
    groups, members, rows, columns, steps, halves, blocks = dims
    bits = columns.bit_length() - 1
    height = rows * groups
    f = lax.axis_index("freq")
    t = lax.axis_index("tmpl")
    flipped = t + 2 - 4 * ((t // 2) % 2)
    sibling = t + 1 - 2 * (t % 2)
    pairs = members // 2
    slot = (t % 2) * pairs + t // 2
    my_half = f // blocks
    my_block = f % blocks

    def partner(j):
        return ((f // 4 + j // 4) % 4) * 4 + (f % 4 + j % 4) % 4

    strain_copy = pltpu.make_async_copy(strain_ref, strain, strain_sem)
    strain_copy.start()
    barrier = pltpu.get_barrier_semaphore()

    def greet_partner(j, carry):
        pl.semaphore_signal(barrier, inc=1, device_id=(partner(j), flipped), device_id_type=MESH)
        return carry

    def greet_member(j, carry):
        pl.semaphore_signal(barrier, inc=1, device_id=(f, (t + 2 * j) % members), device_id_type=MESH)
        return carry

    lax.fori_loop(1, groups, greet_partner, 0)
    lax.fori_loop(1, pairs, greet_member, 0)
    pl.semaphore_signal(barrier, inc=1, device_id=(f, sibling), device_id_type=MESH)

    bank_copy = pltpu.make_async_copy(bank_ref, bank, bank_sem)
    bank_copy.start()

    row, col = iotas((rows, columns))
    near_c[...], near_s[...] = unit_circle((row * col) & (columns - 1), bits)
    row, col = iotas((groups, columns))
    far_c[...], far_s[...] = unit_circle((row * col * rows) & (columns - 1), bits)

    def table(h, carry):
        fc = far_c[pl.ds(h, 1), :]
        fs = far_s[pl.ds(h, 1), :]
        nc = near_c[...]
        ns = near_s[...]
        at = pl.ds(pl.multiple_of(h * rows, rows), rows)
        cos_table[at, :] = (nc * fc - ns * fs).astype(jnp.bfloat16)
        sin_table[at, :] = (ns * fc + nc * fs).astype(jnp.bfloat16)
        return carry

    strain_copy.wait()
    packed[...] = jnp.concatenate([strain[0], strain[1]], axis=1)
    pl.semaphore_wait(barrier, groups - 1 + pairs)

    def send_strain(j, carry):
        pltpu.make_async_remote_copy(
            src_ref=packed,
            dst_ref=gathered.at[slot],
            send_sem=strain_send,
            recv_sem=strain_recv.at[j],
            device_id=(f, (t + 2 * j) % members),
            device_id_type=MESH,
        ).start()
        return carry

    lax.fori_loop(1, pairs, send_strain, 0)
    pltpu.make_async_remote_copy(
        src_ref=packed,
        dst_ref=gathered.at[slot],
        send_sem=strain_send,
        recv_sem=sibling_recv,
        device_id=(f, sibling),
        device_id_type=MESH,
    ).start()
    gathered[slot] = packed[...]
    per_pair = groups // pairs
    lax.fori_loop(0, per_pair, table, 0)

    def forward(j, carry):
        lax.fori_loop(per_pair * j, per_pair * (j + 1), table, 0)
        source = (t - 2 * j + members) % members
        block = gathered.at[(t % 2) * pairs + source // 2]
        pltpu.make_async_copy(block, block, strain_recv.at[j]).wait()
        pltpu.make_async_remote_copy(
            src_ref=block,
            dst_ref=block,
            send_sem=strain_send,
            recv_sem=sibling_recv,
            device_id=(f, sibling),
            device_id_type=MESH,
        ).start()
        return carry

    lax.fori_loop(1, pairs, forward, 0)

    row, col = iotas((rows, columns))
    turn_c[...], turn_s[...] = unit_circle((f * rows + row) * col, 2 * bits)

    sent = gathered.at[pl.ds(0, members - 1)]
    half = gathered.at[pl.ds(pl.multiple_of((1 - t % 2) * pairs, pairs), pairs)]
    pltpu.make_async_copy(half, half, sibling_recv).wait()
    lane = lax.broadcasted_iota(jnp.int32, (rows, LANES), 1)
    low = lane < LANES // 2
    for pair in range(members // 2):
        first = gathered[pair]
        second = gathered[pairs + pair]
        at = pl.ds(pair * LANES, LANES)
        strain_re[:, at] = jnp.where(low, first, pltpu.roll(second, LANES // 2, 1))
        strain_im[:, at] = jnp.where(low, pltpu.roll(first, LANES // 2, 1), second)
    bank_copy.wait()

    def first_pass(i, carry):
        sr = strain_re[...]
        si = strain_im[...]
        for h in range(halves):
            hr = bank[h * steps + i, 0].astype(jnp.float32)
            hi = bank[h * steps + i, 1].astype(jnp.float32)
            product[pl.ds(h * rows, rows), :] = (sr * hr + si * hi).astype(jnp.bfloat16)
            product[pl.ds((halves + h) * rows, rows), :] = (si * hr - sr * hi).astype(jnp.bfloat16)

        def columns_of(j, inner):
            n = (my_block // 2 + j) % (columns // CHUNK)
            at = pl.ds(pl.multiple_of(n * CHUNK, CHUNK), CHUNK)
            with_cos = jnp.dot(product[...], cos_table[:, at], preferred_element_type=jnp.float32)
            with_sin = jnp.dot(product[...], sin_table[:, at], preferred_element_type=jnp.float32)
            tc = turn_c[:, at]
            ts = turn_s[:, at]
            for h in range(halves):
                up = slice(h * rows, (h + 1) * rows)
                down = slice((halves + h) * rows, (halves + h + 1) * rows)
                re = with_cos[up] - with_sin[down]
                im = with_sin[up] + with_cos[down]
                turned_re = (re * tc - im * ts).astype(jnp.bfloat16)
                turned_im = (re * ts + im * tc).astype(jnp.bfloat16)
                for q in range(CHUNK // LANES):
                    piece = slice(q * LANES, (q + 1) * LANES)
                    d = h * blocks + n * (CHUNK // LANES) + q
                    turned[i, d, :, :LANES] = turned_re[:, piece]
                    turned[i, d, :, LANES:] = turned_im[:, piece]
            for h in range(halves):
                for q in range(CHUNK // LANES):
                    d = h * blocks + n * (CHUNK // LANES) + q
                    pltpu.make_async_remote_copy(
                        src_ref=turned.at[i, d],
                        dst_ref=spectra.at[i, pl.ds(pl.multiple_of(f * rows, rows), rows)],
                        send_sem=turned_send.at[i],
                        recv_sem=turned_recv.at[i],
                        device_id=(d, flipped),
                        device_id_type=MESH,
                    ).start()
            return inner

        lax.fori_loop(0, columns // CHUNK, columns_of, 0)
        return carry

    lax.fori_loop(0, steps, first_pass, 0)

    def second_pass(i, carry):
        here = spectra.at[i]
        pltpu.make_async_copy(here, here, turned_recv.at[i]).wait()

        def rows_of(n, inner):
            at = pl.ds(pl.multiple_of(n * CHUNK, CHUNK), CHUNK)
            with_cos = jnp.dot(cos_table[at, :], spectra[i], preferred_element_type=jnp.float32)
            with_sin = jnp.dot(sin_table[at, :], spectra[i], preferred_element_type=jnp.float32)
            re = with_cos[:, :LANES] - with_sin[:, LANES:]
            im = with_sin[:, :LANES] + with_cos[:, LANES:]
            power = re * re + im * im
            energy[i, at, :] = power.astype(jnp.bfloat16)
            for q in range(CHUNK // rows):
                top = power[q * rows : q * rows + 1]
                bottom = power[(q + 1) * rows - 1 : (q + 1) * rows]
                edges[i, n * (CHUNK // rows) + q] = jnp.where(my_block == 0, top, bottom)
            return inner

        lax.fori_loop(0, height // CHUNK, rows_of, 0)

        def send(j, inner):
            d = partner(j)
            pltpu.make_async_remote_copy(
                src_ref=energy.at[i, pl.ds(pl.multiple_of(d * rows, rows), rows)],
                dst_ref=series.at[i, f],
                send_sem=energy_send.at[i],
                recv_sem=energy_recv.at[i],
                device_id=(d, flipped),
                device_id_type=MESH,
            ).start()

            @pl.when((my_block == 0) | (my_block == blocks - 1))
            def _():
                side = 1 - my_block // (blocks - 1)
                pltpu.make_async_remote_copy(
                    src_ref=edges.at[i, (d + groups - 1 + 2 * side) % groups],
                    dst_ref=halo.at[i, my_half, side],
                    send_sem=halo_send.at[i],
                    recv_sem=halo_recv.at[i],
                    device_id=(d, flipped),
                    device_id_type=MESH,
                ).start()

            return inner

        lax.fori_loop(0, groups, send, 0)
        return carry

    lax.fori_loop(0, steps, second_pass, 0)

    def window(i, carry):
        here = series.at[i]
        pltpu.make_async_copy(here, here, energy_recv.at[i]).wait()
        outer = halo.at[i]
        pltpu.make_async_copy(outer, outer, halo_recv.at[i]).wait()

        def one(h, inner):
            before = jnp.broadcast_to(halo[i, h, 0], (8, LANES))
            after = jnp.broadcast_to(halo[i, h, 1], (8, LANES))
            tiles = [series[i, h * blocks + b].astype(jnp.float32) for b in range(blocks)]
            follow = jnp.concatenate([after, tiles[0], after], axis=0)
            follow = pltpu.roll(follow, rows + 15, 0)[: rows + 8]
            tiles = [jnp.concatenate([before, tile], axis=0) for tile in tiles] + [follow]
            place = lax.broadcasted_iota(jnp.int32, (rows + 8, LANES), 1)
            stride = 1
            while stride < LANES:
                moved = [pltpu.roll(tile, LANES - stride, 1) for tile in tiles]
                inside = place < LANES - stride
                tiles = [
                    jnp.maximum(tiles[b], jnp.where(inside, moved[b], moved[b + 1])) for b in range(blocks)
                ] + [jnp.maximum(tiles[blocks], moved[blocks])]
                stride *= 2
            ahead = pltpu.roll(tiles[blocks - 1], 1, 0)[8:]
            for b in range(blocks):
                peak = jnp.maximum(ahead, tiles[b][8:])
                ahead = tiles[b][8:]
                result[pl.ds(b * 8 + h * steps + i, rows, stride=8 * blocks), :] = peak
            return inner

        lax.fori_loop(0, halves, one, 0)
        return carry

    lax.fori_loop(0, steps, window, 0)

    pltpu.make_async_copy(sent, sent, strain_send).wait()

    def drain(i, carry):
        out = turned.at[i]
        pltpu.make_async_copy(out, out, turned_send.at[i]).wait()
        out = series.at[i]
        pltpu.make_async_copy(out, out, energy_send.at[i]).wait()

        @pl.when((my_block == 0) | (my_block == blocks - 1))
        def _():
            edge = edges.at[i]
            pltpu.make_async_copy(edge, edge, halo_send.at[i]).wait()

        return carry

    lax.fori_loop(0, steps, drain, 0)


def shards(groups, members, strain_spectrum, bank_spectra):
    templates, _, rows, columns = bank_spectra.shape
    blocks = columns // LANES
    halves = groups // blocks
    steps = templates // halves
    height = rows * groups
    dims = (groups, members, rows, columns, steps, halves, blocks)
    f32, bf16 = jnp.float32, jnp.bfloat16
    dma = pltpu.SemaphoreType.DMA
    out = pl.pallas_call(
        functools.partial(kernel, dims),
        out_shape=jax.ShapeDtypeStruct((rows * blocks * templates, LANES), f32),
        in_specs=[pl.BlockSpec(memory_space=pltpu.HBM)] * 2,
        out_specs=pl.BlockSpec(memory_space=pltpu.VMEM),
        scratch_shapes=[
            pltpu.VMEM((2, rows, columns // members), f32),
            pltpu.VMEM((templates, 2, rows, columns), bf16),
            pltpu.VMEM((rows, columns), f32),
            pltpu.VMEM((rows, columns), f32),
            pltpu.VMEM((groups, columns), f32),
            pltpu.VMEM((groups, columns), f32),
            pltpu.VMEM((columns, columns), bf16),
            pltpu.VMEM((columns, columns), bf16),
            pltpu.VMEM((rows, columns), f32),
            pltpu.VMEM((rows, columns), f32),
            pltpu.VMEM((rows, LANES), f32),
            pltpu.VMEM((members, rows, LANES), f32),
            pltpu.VMEM((rows, columns), f32),
            pltpu.VMEM((rows, columns), f32),
            pltpu.VMEM((2 * halves * rows, columns), bf16),
            pltpu.VMEM((steps, groups, rows, 2 * LANES), bf16),
            pltpu.VMEM((steps, height, 2 * LANES), bf16),
            pltpu.VMEM((steps, height, LANES), bf16),
            pltpu.VMEM((steps, groups, rows, LANES), bf16),
            pltpu.VMEM((steps, groups, 1, LANES), f32),
            pltpu.VMEM((steps, halves, 2, 1, LANES), f32),
            dma,
            dma,
            dma,
            dma((members // 2,)),
            dma,
            dma((steps,)),
            dma((steps,)),
            dma((steps,)),
            dma((steps,)),
            dma((steps,)),
            dma((steps,)),
        ],
        compiler_params=pltpu.CompilerParams(
            collective_id=0, has_side_effects=True, vmem_limit_bytes=40 * 2**20
        ),
    )(*[pltpu.with_memory_space_constraint(x, pltpu.HBM) for x in (strain_spectrum, bank_spectra)])
    out = out.reshape(rows * blocks, templates, LANES).transpose(1, 0, 2)
    return out.reshape(templates, rows * columns)


def solution(mesh):
    body = functools.partial(shards, mesh.shape["freq"], mesh.shape["tmpl"])
    in_specs = (P(None, "freq", "tmpl"), P("tmpl", None, "freq", None))
    return jax.shard_map(body, mesh=mesh, in_specs=in_specs, out_specs=P("tmpl", "freq"), check_vma=False)
```
